512 devices in a mesh: grp: 16 (over x_lo, y), blk: 32 (over x_hi, z, core).
Axes of the slice: x: 4 (x_hi: 2, x_lo: 2; x = x_hi * 2 + x_lo), y: 8, z: 8, core: 2. Of those that a mesh axis runs over, the one named last changes fastest.
Arguments:
- walkers: bfloat16 [128, 128, 768], P('blk', 'grp'), may hold values from -6 to 6
- one_body: bfloat16 [768, 768], replicated, may hold values from -0.21875 to 0.21875
- fields: float32 [128, 384], P('grp', 'blk'), may hold values from -6 to 6
- field_diag: float32 [384, 768], P('blk'), may hold values from -0.4375 to 0.4375
- chol: bfloat16 [384, 128, 768], P('blk'), may hold values from -0.1875 to 0.1875
- weights: float32 [128], P('grp'), may hold values from 0.25 to 12, as said below
- target: int32 [128], P('grp'), may hold values from 0 to 64, as said below
Outputs:
- fock: bfloat16 [128, 128, 768], P('blk', 'grp')
The draws below stay inside these ranges and needn't reach their ends.
Inputs may be any that keep to these rules, and one draw needn't show every extreme that they name: `target`: each list of 8 slots (the slots of one index of grp) holds its live walkers in its first slots. The live walkers of all lists, in order of list and slot, carry the numbers 0 to 63, each once; a dead slot holds 64. A list holds 0 to 8 live walkers, and some list holds exactly 8. `weights`: Positive.
All inputs are finite; a program needn't handle non-finite values.
Results may differ from the reference program's by a relative error of at most 0.018.
Values may be sent and summed in bfloat16 or wider, within the bound.
A program may use at most 64 MiB of HBM per device.

```python
import math
import jax
import jax.numpy as jnp
from jax import lax

NOCC = 128
NORB = 768
SLOTS = 8
WALKERS = 128
LIVE = 64
NCHOL = 384


def draw_target(key, part):
    groups = WALKERS // SLOTS
    first_key, second_key = jax.random.split(jax.random.fold_in(key, 11))
    halves = jax.random.randint(first_key, (groups // 2,), 0, SLOTS + 1)
    halves = halves.at[0].set(SLOTS)
    counts = jnp.stack([halves, SLOTS - halves], axis=1).reshape(groups)
    counts = jax.random.permutation(second_key, counts)
    starts = jnp.cumsum(counts) - counts
    position = jnp.arange(SLOTS)
    target = jnp.where(position[None, :] < counts[:, None], starts[:, None] + position[None, :], LIVE)
    return target.reshape(WALKERS).astype(jnp.int32)


def draw_weights(key, part):
    groups = WALKERS // SLOTS
    sample_key = jax.random.fold_in(key, 23)
    sample = jnp.exp(jax.random.uniform(sample_key, (WALKERS,), jnp.float32, math.log(0.5), math.log(2.0)))
    rising = 3.0 ** (jnp.arange(WALKERS) // SLOTS / max(groups - 1, 1))
    return (sample * rising).astype(jnp.float32)


def levels(key, dims, pieces, smallest, high):
    loudness = 1.0
    for dim, blocks in pieces:
        heights = jax.random.uniform(jax.random.fold_in(jax.random.fold_in(key, 6), dim), (blocks,), jnp.float32, smallest / len(pieces), high / len(pieces))
        loudness = loudness * jnp.repeat(jnp.exp(heights), dims[dim] // blocks).reshape((-1,) + (1,) * (len(dims) - 1 - dim))
    return loudness


def noise(key, shape, spread, limit, cuts=(), held_as=jnp.bfloat16):
    gain = levels(key, shape, cuts, -0.22, 0.18) if cuts else 1.0
    drawn = jax.random.normal(key, shape, jnp.float32) * spread * gain
    return jnp.minimum(jnp.maximum(drawn, -limit), limit).astype(held_as)


def setup_inputs(seed: int = 0) -> dict:
    keys = jax.random.split(jax.random.key(seed), 8)
    walkers = noise(keys[0], (NOCC, WALKERS, NORB), 1.0, 6.0, ((0, 32), (1, 16)))
    one_body = noise(keys[1], (NORB, NORB), NORB ** -0.5, 0.21875)
    fields = noise(keys[2], (WALKERS, NCHOL), 1.0, 6.0, ((0, 16), (1, 32)), jnp.float32)
    field_diag = noise(keys[3], (NCHOL, NORB), (0.6 * NCHOL ** -0.5), 0.4375, ((0, 32),), jnp.float32)
    chol = noise(keys[4], (NCHOL, NOCC, NORB), ((NORB * NOCC * NCHOL) ** -0.25), 0.1875, ((0, 32),))
    weights = draw_weights(jax.random.fold_in(keys[7], 71), 0)
    target = draw_target(jax.random.fold_in(keys[7], 71), 0)
    return {"walkers": walkers, "one_body": one_body, "fields": fields, "field_diag": field_diag, "chol": chol, "weights": weights, "target": target}


def reference(walkers, one_body, fields, field_diag, chol, weights, target):
    exponent = jnp.dot(fields, field_diag, precision=lax.Precision.HIGHEST)
    scaled = (walkers.astype(jnp.float32) * jnp.exp(exponent)[None]).astype(jnp.bfloat16)
    propagated = jnp.dot(scaled.reshape(-1, NORB), one_body, preferred_element_type=jnp.float32)
    propagated = propagated.astype(jnp.bfloat16).reshape(NOCC, WALKERS, NORB)
    vectors = chol.reshape(NCHOL * NOCC, NORB)

    def measure(walker_block):
        coupling = lax.dot_general(walker_block, vectors, (((1,), (1,)), ((), ())), preferred_element_type=jnp.float32)
        coupling = coupling.astype(jnp.bfloat16).reshape(NOCC, NCHOL, NOCC)
        flipped = jnp.transpose(coupling, (2, 1, 0)).reshape(NOCC, NCHOL * NOCC)
        return jnp.dot(flipped, vectors, preferred_element_type=jnp.float32).astype(jnp.bfloat16)

    fock_raw = lax.map(measure, jnp.transpose(propagated, (1, 0, 2)))
    fock_raw = lax.optimization_barrier(jnp.transpose(fock_raw, (1, 0, 2)))
    active = target < LIVE
    weight_sum = jnp.sum(jnp.where(active, weights, jnp.float32(0.0)))
    factor = jnp.where(active, weights * LIVE / weight_sum, jnp.float32(0.0))
    return (fock_raw.astype(jnp.float32) * factor[None, :, None]).astype(jnp.bfloat16)
```

```python
import jax
import jax.numpy as jnp
from jax import lax
from jax.experimental import pallas as pl
from jax.experimental.pallas import tpu as pltpu
from jax.sharding import PartitionSpec as P

MESH = pl.DeviceIdType.MESH
F32 = jnp.float32
BF16 = jnp.bfloat16

NZ = 8
NY = 8
SLOTS = 8
HALF = SLOTS // 2
ROWS = 4
QUAD = 4
ZROWS = QUAD * ROWS
NOCC = NZ * ZROWS
NORB = 768
LANES = NORB // 128
VEC = 12
TV = 6
LIVE = 64


def far(walker):
    up = 4 if walker < HALF // 2 else 3
    return up, NZ - 1 - up


def kernel(
    walkers, one_body, fields, field_diag, chol, weights, target, out,
    X, S, G, FI, FD, EP, ER, E, ET, OB, CH, PR, LH, F, RS, RR, T, PC, FR, O, OW, WS, WX, WR,
    loc, qs, qr, es, er, ws, wr, gs, gr, ss, sr, fs, fr,
):
    p = lax.axis_index("grp")
    b = lax.axis_index("blk")
    x_lo, y = p // NY, p % NY
    x_hi, z, c = b // (2 * NZ), (b // 2) % NZ, b % 2
    q_me = x_hi * 2 + c

    def at_blk(xh, zz, cc):
        return {"blk": xh * (2 * NZ) + zz * 2 + cc}

    quad = {
        k: at_blk(x_hi ^ 1 if k & 2 else x_hi, z, c ^ 1 if k & 1 else c) for k in (1, 2, 3)
    }
    z_dev = (at_blk(x_hi, (z + 1) % NZ, c), at_blk(x_hi, (z + NZ - 1) % NZ, c))
    y_dev = ({"grp": x_lo * NY + (y + 1) % NY}, {"grp": x_lo * NY + (y + NY - 1) % NY})
    x_dev = {"grp": (x_lo ^ 1) * NY + y}

    def rcopy(src, dst, s, r, dev):
        return pltpu.make_async_remote_copy(
            src_ref=src, dst_ref=dst, send_sem=s, recv_sem=r, device_id=dev, device_id_type=MESH
        )

    local = [
        pltpu.make_async_copy(fields, FI, loc.at[0]),
        pltpu.make_async_copy(field_diag, FD, loc.at[1]),
        pltpu.make_async_copy(walkers, X.at[q_me], loc.at[2]),
        pltpu.make_async_copy(one_body, OB, loc.at[3]),
        pltpu.make_async_copy(chol.at[:, 0], CH.at[pl.ds(0, VEC), :, 0], loc.at[4]),
        pltpu.make_async_copy(chol.at[:, 1], CH.at[pl.ds(0, VEC), :, 1], loc.at[5]),
    ]
    for copy in local:
        copy.start()

    barrier = pltpu.get_barrier_semaphore()
    partners = list(quad.values()) + list(z_dev) + list(y_dev) + [x_dev]
    for dev in partners:
        pl.semaphore_signal(barrier, inc=1, device_id=dev, device_id_type=MESH)

    local[0].wait()
    local[1].wait()
    part = FI[:, 0:1] * FD[0:1, :]
    for k in range(1, VEC):
        part += FI[:, k : k + 1] * FD[k : k + 1, :]
    EP[0] = part[:HALF]
    EP[1] = part[HALF:]

    own = jnp.float32(0.0)
    for s in range(SLOTS):
        own = own + jnp.where(target[s] < LIVE, weights[s], jnp.float32(0.0))
    WS[...] = jnp.full((8, 128), own, F32)

    pl.semaphore_wait(barrier, len(partners))

    e_quad = [rcopy(EP.at[c ^ 1 if k & 1 else c], ER.at[k - 1], es.at[k - 1], er.at[k - 1], quad[k]) for k in (2, 3, 1)]
    x_quad = [rcopy(walkers, X.at[q_me], qs.at[k - 1], qr.at[k - 1], quad[k]) for k in (2, 3, 1)]
    for copy in e_quad + x_quad:
        copy.start()
    w_pair = rcopy(WS, WX, ws.at[0], wr.at[0], x_dev)
    w_pair.start()
    c_pair = [
        rcopy(chol.at[:, h], CH.at[pl.ds(VEC, VEC), :, h], fs.at[h], fr.at[h], quad[1])
        for h in range(2)
    ]
    for copy in c_pair:
        copy.start()

    def item(view, me, devs, send, recv, steps):
        def block(way, hop):
            return (me - hop) % 8 if way == 0 else (me + hop) % 8

        def copy(way, step):
            ref = view(block(way, step - 1))
            return rcopy(ref, ref, send.at[way, step - 1], recv.at[way, step - 1], devs[way])

        def arrived(way, step):
            ref = view(block(way, step))
            rcopy(ref, ref, send.at[way, step - 1], recv.at[way, step - 1], devs[way]).wait_recv()

        return copy, arrived, steps

    items = [item(lambda i: E.at[i], z, z_dev, gs.at[HALF], gr.at[HALF], (4, 3))]
    for w in range(HALF):
        items.append(item(lambda i, w=w: G.at[w, i], z, z_dev, gs.at[w], gr.at[w], far(w)))
    items.append(item(lambda i: WR.at[i], y, y_dev, gs.at[HALF + 1], gr.at[HALF + 1], (4, 3)))
    sent = []

    def start(it, step):
        copy, _, steps = it
        for way in range(2):
            if step <= steps[way]:
                cp = copy(way, step)
                cp.start()
                sent.append(cp)

    def forward(it, step):
        copy, arrived, steps = it
        for way in range(2):
            if step <= steps[way]:
                arrived(way, step)
                if step + 1 <= steps[way]:
                    cp = copy(way, step + 1)
                    cp.start()
                    sent.append(cp)

    for copy in e_quad:
        copy.wait_recv()
    E[z] = (EP[c] + ER[1]) + (ER[0] + ER[2])
    start(items[0], 1)

    local[2].wait()
    for copy in x_quad:
        copy.wait_recv()
    for q in range(QUAD):
        for r in range(ROWS):
            rows = X[q, r].astype(F32)
            for n in range(LANES):
                S[n, pl.ds((q * ROWS + r) * SLOTS, SLOTS), :] = rows[:, n * 128 : (n + 1) * 128]
    for w in range(HALF):
        for n in range(LANES):
            lo = S[n, pl.ds(w, ZROWS, stride=SLOTS), :]
            hi = S[n, pl.ds(HALF + w, ZROWS, stride=SLOTS), :]
            G[w, z, :, n * 128 : (n + 1) * 128] = jnp.where(c == 0, lo, hi).astype(BF16)
        start(items[1 + w], 1)

    w_pair.wait_recv()
    WR[y] = WS[...] + WX[...]
    start(items[-1], 1)

    for step in range(1, 5):
        for it in items:
            forward(it, step)

    total = E[0]
    for i in range(1, NZ):
        total += E[i]
    ET[...] = jnp.exp(total)

    total = WR[0]
    for i in range(1, NY):
        total += WR[i]
    row = lax.broadcasted_iota(jnp.int32, (8, 128), 0)
    factor = jnp.zeros((8, 128), F32)
    for s in range(SLOTS):
        mine = jnp.where(target[s] < LIVE, weights[s] * LIVE, jnp.float32(0.0))
        factor = jnp.where(row == s, mine, factor)
    WS2 = factor / total

    local[3].wait()
    for copy in local[4:]:
        copy.wait()
    for copy in c_pair:
        copy.wait_recv()

    vectors = CH.reshape(2 * VEC * NOCC, NORB)

    rs_sent = []

    def rs_step(w, step):
        for way in range(2):
            depth = far(w)[way]
            if step > depth:
                continue
            hop = depth - step + 1
            zz = (z + hop) % NZ if way == 0 else (z + NZ - hop) % NZ
            rows = F[pl.ds(pl.multiple_of(w * NOCC + zz * ZROWS, ZROWS), ZROWS), :]
            if step > 1:
                slot = RR.at[w, way, step - 2]
                rcopy(slot, slot, ss.at[w, way, step - 2], sr.at[w, way, step - 2], z_dev[way]).wait_recv()
                rows = rows + RR[w, way, step - 2].astype(F32)
            RS[w, way, step - 1] = rows.astype(BF16)
            cp = rcopy(
                RS.at[w, way, step - 1], RR.at[w, way, step - 1],
                ss.at[w, way, step - 1], sr.at[w, way, step - 1], z_dev[way],
            )
            cp.start()
            rs_sent.append(cp)

    def compute(pair, hooks):
        base = pair * 2 * NOCC
        for w in range(2):
            wk = pair * 2 + w
            rows = G[wk].reshape(NOCC, NORB).astype(F32) * ET[wk : wk + 1, :]
            PR[w * NOCC : (w + 1) * NOCC, :] = rows.astype(BF16)
        prop = jnp.dot(PR[...], OB[...], preferred_element_type=F32).astype(BF16)
        PR[...] = prop
        for t in range(2 * VEC // TV):
            res = lax.dot_general(
                vectors[t * TV * NOCC : (t + 1) * TV * NOCC, :], PR[...],
                (((1,), (1,)), ((), ())), preferred_element_type=F32,
            ).astype(BF16)
            for g in range(TV):
                for w in range(2):
                    LH[w * NOCC : (w + 1) * NOCC, (t * TV + g) * NOCC : (t * TV + g + 1) * NOCC] = res[
                        g * NOCC : (g + 1) * NOCC, w * NOCC : (w + 1) * NOCC
                    ]
            if t == 1 and hooks:
                hooks.pop(0)()
        if hooks:
            hooks.pop(0)()
        for n in range(NORB // 256):
            F[base : base + 2 * NOCC, n * 256 : (n + 1) * 256] = jnp.dot(
                LH[...], vectors[:, n * 256 : (n + 1) * 256], preferred_element_type=F32
            )
            if n == 0 and hooks:
                hooks.pop(0)()

    def both(pair, step):
        for w in range(2):
            rs_step(pair * 2 + w, step)

    compute(0, [])
    both(0, 1)
    compute(1, [lambda s=s: both(0, s) for s in (2, 3, 4)])
    both(1, 1)
    for step in (2, 3, 4):
        both(1, step)

    for w in range(HALF):
        rows = F[pl.ds(pl.multiple_of(w * NOCC + z * ZROWS, ZROWS), ZROWS), :]
        for way in range(2):
            last = far(w)[way] - 1
            slot = RR.at[w, way, last]
            rcopy(slot, slot, ss.at[w, way, last], sr.at[w, way, last], z_dev[way]).wait_recv()
            rows = rows + RR[w, way, last].astype(F32)
        for n in range(LANES):
            T[n, w * ZROWS : (w + 1) * ZROWS, :] = rows[:, n * 128 : (n + 1) * 128]
    for q in range(QUAD):
        for r in range(ROWS):
            for n in range(LANES):
                PC[q, r, :, n * 128 : (n + 1) * 128] = T[
                    n, pl.ds(q * ROWS + r, HALF, stride=ZROWS), :
                ].astype(BF16)
    fin = [rcopy(PC.at[q_me ^ k], FR.at[k - 1], fs.at[1 + k], fr.at[1 + k], quad[k]) for k in (3, 2, 1)]
    for copy in fin:
        copy.start()
    for copy in fin:
        copy.wait_recv()
    O[c] = PC[q_me].astype(F32) + FR[1].astype(F32)
    O[c ^ 1] = FR[0].astype(F32) + FR[2].astype(F32)
    scale = WS2[:, 0:1]
    for r in range(ROWS):
        OW[r, 0:HALF, :] = O[0, r]
        OW[r, HALF:SLOTS, :] = O[1, r]
        out[r] = (OW[r].astype(BF16).astype(F32) * scale).astype(BF16)

    for copy in e_quad + x_quad + [w_pair] + c_pair + sent + rs_sent + fin:
        copy.wait_send()


def body(walkers, one_body, fields, field_diag, chol, weights, target):
    vmem, sem = pltpu.VMEM, pltpu.SemaphoreType.DMA
    any_, smem = pl.BlockSpec(memory_space=pl.ANY), pl.BlockSpec(memory_space=pltpu.SMEM)
    return pl.pallas_call(
        kernel,
        out_shape=jax.ShapeDtypeStruct((ROWS, SLOTS, NORB), BF16),
        in_specs=[any_] * 5 + [smem] * 2,
        out_specs=pl.BlockSpec(memory_space=pltpu.VMEM),
        scratch_shapes=[
            vmem((QUAD, ROWS, SLOTS, NORB), BF16),
            vmem((LANES, QUAD * ROWS * SLOTS, 128), F32),
            vmem((HALF, NZ, ZROWS, NORB), BF16),
            vmem((SLOTS, VEC), F32),
            vmem((VEC, NORB), F32),
            vmem((2, HALF, NORB), F32),
            vmem((3, HALF, NORB), F32),
            vmem((NZ, HALF, NORB), F32),
            vmem((HALF, NORB), F32),
            vmem((NORB, NORB), BF16),
            vmem((2 * VEC, NZ, 2, 8, NORB), BF16),
            vmem((2 * NOCC, NORB), BF16),
            vmem((2 * NOCC, 2 * VEC * NOCC), BF16),
            vmem((HALF * NOCC, NORB), F32),
            vmem((HALF, 2, 4, ZROWS, NORB), BF16),
            vmem((HALF, 2, 4, ZROWS, NORB), BF16),
            vmem((LANES, HALF * ZROWS, 128), F32),
            vmem((QUAD, ROWS, HALF, NORB), BF16),
            vmem((3, ROWS, HALF, NORB), BF16),
            vmem((2, ROWS, HALF, NORB), F32),
            vmem((ROWS, SLOTS, NORB), F32),
            vmem((8, 128), F32),
            vmem((8, 128), F32),
            vmem((NY, 8, 128), F32),
            sem((6,)),
            sem((3,)), sem((3,)),
            sem((3,)), sem((3,)),
            sem((1,)), sem((1,)),
            sem((HALF + 2, 2, 4)), sem((HALF + 2, 2, 4)),
            sem((HALF, 2, 4)), sem((HALF, 2, 4)),
            sem((5,)), sem((5,)),
        ],
        compiler_params=pltpu.CompilerParams(
            collective_id=0, has_side_effects=True, vmem_limit_bytes=56 * 1024 * 1024
        ),
    )(
        walkers, one_body, fields, field_diag,
        chol.reshape(VEC, 2, NZ, 8, NORB), weights, target,
    )


def solution(mesh):
    in_specs = (
        P("blk", "grp", None),
        P(),
        P("grp", "blk"),
        P("blk", None),
        P("blk", None, None),
        P("grp"),
        P("grp"),
    )
    out_specs = P("blk", "grp", None)
    return jax.shard_map(body, mesh=mesh, in_specs=in_specs, out_specs=out_specs, check_vma=False)
```

```python
import jax
import jax.numpy as jnp
from jax import lax
from jax.experimental import pallas as pl
from jax.experimental.pallas import tpu as pltpu
from jax.sharding import PartitionSpec as P

MESH = pl.DeviceIdType.MESH
F32 = jnp.float32
BF16 = jnp.bfloat16

NZ = 8
NY = 8
SLOTS = 8
HALF = SLOTS // 2
ROWS = 4
QUAD = 4
ZROWS = QUAD * ROWS
NOCC = NZ * ZROWS
NORB = 768
LANES = NORB // 128
VEC = 12
TV = 6
LIVE = 64
ORDER = (2, 1, 3, 0)

RING = (0, 1, 7, 2, 6, 3, 5, 4)


def kernel(
    walkers, one_body, fields, field_diag, chol, weights, target, out,
    XW, WP, GP, S, FI, FD, EP, ER, E, ET, OB, CH, CP, PR, LH, F, XS, XR, T, ZS, ZR, V, U,
    WS, WX, WR,
    loc, es, er, e2s, e2r, ws, wr, ys, yr, cs, cr, gs, gr, xs, xr, rxs, rxr, rzs, rzr,
):
    p = lax.axis_index("grp")
    b = lax.axis_index("blk")
    x_lo, y = p // NY, p % NY
    x_hi, z, c = b // (2 * NZ), (b // 2) % NZ, b % 2
    x_other = x_hi ^ 1

    def at_blk(xh, zz, cc):
        return {"blk": xh * (2 * NZ) + zz * 2 + cc}

    quad = {
        k: at_blk(x_hi ^ 1 if k & 2 else x_hi, z, c ^ 1 if k & 1 else c) for k in (1, 2, 3)
    }
    column = {
        (d, k): at_blk(x_hi, (z + d) % NZ, c ^ k) for d in RING for k in range(2) if d or k
    }
    y_dev = ({"grp": x_lo * NY + (y + 1) % NY}, {"grp": x_lo * NY + (y + NY - 1) % NY})
    x_dev = {"grp": (x_lo ^ 1) * NY + y}
    started = []

    def rcopy(src, dst, s, r, dev):
        return pltpu.make_async_remote_copy(
            src_ref=src, dst_ref=dst, send_sem=s, recv_sem=r, device_id=dev, device_id_type=MESH
        )

    def send(src, dst, s, r, dev):
        copy = rcopy(src, dst, s, r, dev)
        copy.start()
        started.append(copy)

    def arrived(ref, s, r):
        rcopy(ref, ref, s, r, quad[1]).wait_recv()

    local = [
        pltpu.make_async_copy(walkers, XW, loc.at[0]),
        pltpu.make_async_copy(fields, FI, loc.at[1]),
        pltpu.make_async_copy(field_diag, FD, loc.at[2]),
        pltpu.make_async_copy(one_body, OB, loc.at[3]),
        pltpu.make_async_copy(chol, CH.at[0], loc.at[4]),
    ]
    for copy in local:
        copy.start()

    barrier = pltpu.get_barrier_semaphore()
    partners = list(column.values()) + [quad[2], quad[3]] + list(y_dev) + [x_dev]
    for dev in partners:
        pl.semaphore_signal(barrier, inc=1, device_id=dev, device_id_type=MESH)

    local[0].wait()
    low = lax.broadcasted_iota(jnp.int32, (SLOTS, NORB), 0) < HALF
    for r in range(0, ROWS, 2):
        one, two = XW[r].astype(F32), XW[r + 1].astype(F32)
        first = jnp.where(low, one, pltpu.roll(two, HALF, 0))
        second = jnp.where(low, pltpu.roll(one, HALF, 0), two)
        WP[0, r // 2] = first.astype(BF16)
        WP[1, r // 2] = second.astype(BF16)
        GP[x_hi, z, c, r // 2] = jnp.where(c == 0, first, second).astype(BF16)

    local[1].wait()
    local[2].wait()
    part = FI[:, 0:1] * FD[0:1, :]
    for k in range(1, VEC):
        part += FI[:, k : k + 1] * FD[k : k + 1, :]
    EP[0] = part[:HALF]
    EP[1] = part[HALF:]

    own = jnp.float32(0.0)
    for s in range(SLOTS):
        own = own + jnp.where(target[s] < LIVE, weights[s], jnp.float32(0.0))
    WS[...] = jnp.full((8, 128), own, F32)

    pl.semaphore_wait(barrier, len(partners))

    for k in (3, 2, 1):
        send(EP.at[c ^ 1 if k & 1 else c], ER.at[k - 1], es.at[k - 1], er.at[k - 1], quad[k])
    send(WP.at[c], GP.at[x_hi, z, c], xs.at[0, 0], xr.at[0, 0], quad[2])

    def spread(d):
        for k in range(2):
            if d or k:
                send(WP.at[c ^ k], GP.at[x_hi, z, c], gs.at[d, k], gr.at[d, k], column[d, k])

    for d in RING[:5]:
        spread(d)
    send(WS, WX, ws, wr, x_dev)
    send(chol, CH.at[1], cs, cr, quad[1])

    for k in range(3):
        arrived(ER.at[k], es.at[k], er.at[k])
    E[z] = (EP[c] + ER[1]) + (ER[0] + ER[2])
    for d in RING[1:]:
        send(E.at[z], E.at[z], e2s.at[d - 1], e2r.at[d - 1], column[d, 0])
    for d in RING[5:]:
        spread(d)

    def rotate(part, t):
        rows = pl.ds(t * 3 * NOCC, 3 * NOCC)
        flat = CH.at[part].reshape(VEC * NOCC, NORB)
        CP[part, rows, :] = lax.dot_general(
            flat[rows, :], OB[...], (((1,), (1,)), ((), ())), preferred_element_type=F32
        ).astype(BF16)

    def onward(d):
        for k in range(2):
            if d or k:
                ref = GP.at[x_hi, (z + NZ - d) % NZ, c ^ k]
                arrived(ref, gs.at[d, k], gr.at[d, k])
                send(ref, ref, xs.at[d, k], xr.at[d, k], quad[2])

    def weigh(step):
        for way, steps in enumerate((4, 3)):
            if step > 1 and step - 1 <= steps:
                ref = WR.at[(y + NY - step + 1) % NY if way == 0 else (y + step - 1) % NY]
                arrived(ref, ys.at[way, step - 2], yr.at[way, step - 2])
            if step <= steps:
                ref = WR.at[(y + NY - step + 1) % NY if way == 0 else (y + step - 1) % NY]
                send(ref, ref, ys.at[way, step - 1], yr.at[way, step - 1], y_dev[way])

    local[3].wait()
    local[4].wait()
    onward(0)
    rotate(0, 0)
    onward(1)
    onward(7)
    rotate(0, 1)
    onward(2)
    onward(6)
    arrived(WX, ws, wr)
    WR[y] = WS[...] + WX[...]
    weigh(1)
    rotate(0, 2)
    onward(3)
    onward(5)
    rotate(0, 3)
    onward(4)
    weigh(2)
    arrived(CH.at[1], cs, cr)

    for d in RING[1:]:
        arrived(E.at[(z + NZ - d) % NZ], e2s.at[d - 1], e2r.at[d - 1])
    total = E[0]
    for i in range(1, NZ):
        total += E[i]
    grown = jnp.exp(total)
    ET[0:HALF, :] = grown
    ET[HALF:SLOTS, :] = grown

    def scale(xh, d, k):
        zz = (z + NZ - d) % NZ
        base = (xh * 2 * NZ + zz * 2 + (c ^ k)) * ROWS * HALF
        for h in range(2):
            rows = GP[xh, zz, c ^ k, h].astype(F32) * ET[...]
            at = pl.ds(pl.multiple_of(base + h * SLOTS, SLOTS), SLOTS)
            for n in range(LANES):
                S[n, at, :] = rows[:, n * 128 : (n + 1) * 128]

    for i, d in enumerate(RING):
        for k in range(2):
            scale(x_hi, d, k)
        if i % 2:
            rotate(1, i // 2)
    for d in RING:
        for k in range(2):
            arrived(GP.at[x_other, (z + NZ - d) % NZ, c ^ k], xs.at[d, k], xr.at[d, k])
            scale(x_other, d, k)
    weigh(3)
    for w in range(HALF):
        for n in range(LANES):
            PR[w * NOCC : (w + 1) * NOCC, n * 128 : (n + 1) * 128] = S[
                n, pl.ds(w, NOCC, stride=HALF), :
            ].astype(BF16)

    vectors = CH.reshape(2 * VEC * NOCC, NORB)
    rotated = CP.reshape(2 * VEC * NOCC, NORB)

    def compute(pair):
        base = pair * 2 * NOCC
        for t in range(2 * VEC // TV):
            res = lax.dot_general(
                rotated[t * TV * NOCC : (t + 1) * TV * NOCC, :], PR[base : base + 2 * NOCC, :],
                (((1,), (1,)), ((), ())), preferred_element_type=F32,
            ).astype(BF16)
            for g in range(TV):
                for w in range(2):
                    LH[w * NOCC : (w + 1) * NOCC, (t * TV + g) * NOCC : (t * TV + g + 1) * NOCC] = res[
                        g * NOCC : (g + 1) * NOCC, w * NOCC : (w + 1) * NOCC
                    ]
        for n in range(NORB // 256):
            F[base : base + 2 * NOCC, n * 256 : (n + 1) * 256] = jnp.dot(
                LH[...], vectors[:, n * 256 : (n + 1) * 256], preferred_element_type=F32
            )

    def near(k):
        return (z // 2 + k) % (NZ // 2)

    def rows_of(pair, w, xh, zp):
        start = (pair * 2 + w) * NOCC + xh * (NOCC // 2) + zp * ZROWS
        return F[pl.ds(pl.multiple_of(start, ZROWS), ZROWS), :]

    def cross(pair, k):
        for w in range(2):
            XS[pair, k, w] = rows_of(pair, w, x_other, near(k)).astype(BF16)
        send(XS.at[pair, k], XR.at[pair, k], rxs.at[pair, k], rxr.at[pair, k], quad[2])

    def deliver(pair, k):
        arrived(XR.at[pair, k], rxs.at[pair, k], rxr.at[pair, k])
        for w in range(2):
            rows = rows_of(pair, w, x_hi, near(k)) + XR[pair, k, w].astype(F32)
            for n in range(LANES):
                T[pair, k, n, pl.ds(w, ZROWS, stride=2), :] = rows[:, n * 128 : (n + 1) * 128]
        for h in range(2):
            for cc in range(2):
                for n in range(LANES):
                    ZS[pair, k, h, cc, :, n * 128 : (n + 1) * 128] = T[
                        pair, k, n, (h * 2 + cc) * 8 : (h * 2 + cc) * 8 + 8, :
                    ].astype(BF16)
        for t in range(2):
            h = (z % 2) ^ t
            for kc in range(2):
                if k or t or kc:
                    send(
                        ZS.at[pair, k, h, c ^ kc], ZR.at[pair, z, c],
                        rzs.at[pair, k, t, kc], rzr.at[pair, k, t, kc],
                        at_blk(x_hi, near(k) * 2 + h, c ^ kc),
                    )

    def collect(pair):
        for kc in range(2):
            acc = None
            for k in ORDER:
                for t in range(2):
                    zs = ((z // 2 + NZ // 2 - k) % (NZ // 2)) * 2 + ((z % 2) ^ t)
                    if k or t or kc:
                        ref = ZR.at[pair, zs, c ^ kc]
                        arrived(ref, rzs.at[pair, k, t, kc], rzr.at[pair, k, t, kc])
                        rows = ref[...].astype(F32)
                    else:
                        rows = ZS[pair, 0, z % 2, c].astype(F32)
                    acc = rows if acc is None else acc + rows
            at = pl.ds(pl.multiple_of((c ^ kc) * 16 + pair * 8, 8), 8)
            for n in range(LANES):
                V[n, at, :] = acc[:, n * 128 : (n + 1) * 128]

    compute(0)
    for k in ORDER:
        cross(0, k)
    compute(1)
    for k in ORDER:
        cross(1, k)
    weigh(4)
    for pair in range(2):
        for k in ORDER:
            deliver(pair, k)
    weigh(5)
    total = WR[0]
    for i in range(1, NY):
        total += WR[i]
    row = lax.broadcasted_iota(jnp.int32, (8, 128), 0)
    factor = jnp.zeros((8, 128), F32)
    for s in range(SLOTS):
        mine = jnp.where(target[s] < LIVE, weights[s] * LIVE, jnp.float32(0.0))
        factor = jnp.where(row == s, mine, factor)
    factor = factor / total

    for pair in range(2):
        collect(pair)
    for slot in range(SLOTS):
        for n in range(LANES):
            U[n, pl.ds(slot, ROWS, stride=SLOTS), :] = V[
                n, pl.ds((slot // 2) * 8 + slot % 2, ROWS, stride=2), :
            ]
    for r in range(ROWS):
        for n in range(LANES):
            raw = U[n, r * SLOTS : (r + 1) * SLOTS, :].astype(BF16).astype(F32)
            out[r, :, n * 128 : (n + 1) * 128] = (raw * factor).astype(BF16)

    for copy in started:
        copy.wait_send()


def body(walkers, one_body, fields, field_diag, chol, weights, target):
    vmem, sem = pltpu.VMEM, pltpu.SemaphoreType.DMA
    any_, smem = pl.BlockSpec(memory_space=pl.ANY), pl.BlockSpec(memory_space=pltpu.SMEM)
    return pl.pallas_call(
        kernel,
        out_shape=jax.ShapeDtypeStruct((ROWS, SLOTS, NORB), BF16),
        in_specs=[any_] * 5 + [smem] * 2,
        out_specs=pl.BlockSpec(memory_space=pltpu.VMEM),
        scratch_shapes=[
            vmem((ROWS, SLOTS, NORB), BF16),
            vmem((2, 2, SLOTS, NORB), BF16),
            vmem((2, NZ, 2, 2, SLOTS, NORB), BF16),
            vmem((LANES, NOCC * HALF, 128), F32),
            vmem((SLOTS, VEC), F32),
            vmem((VEC, NORB), F32),
            vmem((2, HALF, NORB), F32),
            vmem((3, HALF, NORB), F32),
            vmem((NZ, HALF, NORB), F32),
            vmem((SLOTS, NORB), F32),
            vmem((NORB, NORB), BF16),
            vmem((2, VEC, NOCC, NORB), BF16),
            vmem((2, VEC * NOCC, NORB), BF16),
            vmem((HALF * NOCC, NORB), BF16),
            vmem((2 * NOCC, 2 * VEC * NOCC), BF16),
            vmem((HALF * NOCC, NORB), F32),
            vmem((2, 4, 2, ZROWS, NORB), BF16),
            vmem((2, 4, 2, ZROWS, NORB), BF16),
            vmem((2, 4, LANES, 2 * ZROWS, 128), F32),
            vmem((2, 4, 2, 2, 8, NORB), BF16),
            vmem((2, NZ, 2, 8, NORB), BF16),
            vmem((LANES, 32, 128), F32),
            vmem((LANES, 32, 128), F32),
            vmem((8, 128), F32),
            vmem((8, 128), F32),
            vmem((NY, 8, 128), F32),
            sem((5,)),
            sem((3,)), sem((3,)),
            sem((7,)), sem((7,)),
            sem, sem,
            sem((2, 4)), sem((2, 4)),
            sem, sem,
            sem((NZ, 2)), sem((NZ, 2)),
            sem((NZ, 2)), sem((NZ, 2)),
            sem((2, 4)), sem((2, 4)),
            sem((2, 4, 2, 2)), sem((2, 4, 2, 2)),
        ],
        compiler_params=pltpu.CompilerParams(
            collective_id=0, has_side_effects=True, vmem_limit_bytes=56 * 1024 * 1024
        ),
    )(walkers, one_body, fields, field_diag, chol, weights, target)


def solution(mesh):
    in_specs = (
        P("blk", "grp", None),
        P(),
        P("grp", "blk"),
        P("blk", None),
        P("blk", None, None),
        P("grp"),
        P("grp"),
    )
    out_specs = P("blk", "grp", None)
    return jax.shard_map(body, mesh=mesh, in_specs=in_specs, out_specs=out_specs, check_vma=False)
```

```python
import jax
import jax.numpy as jnp
from jax import lax
from jax.experimental import pallas as pl
from jax.experimental.pallas import tpu as pltpu
from jax.sharding import PartitionSpec as P

MESH = pl.DeviceIdType.MESH
F32 = jnp.float32
BF16 = jnp.bfloat16

NZ = 8
NY = 8
SLOTS = 8
HALF = SLOTS // 2
ROWS = 4
QUAD = 4
ZROWS = QUAD * ROWS
NOCC = NZ * ZROWS
NORB = 768
LANES = NORB // 128
VEC = 12
TV = 6
LIVE = 64

RING = (0, 1, 7, 2, 6, 3, 5, 4)


def kernel(
    walkers, one_body, fields, field_diag, chol, weights, target, out,
    XW, WP, GP, S, FI, FD, EP, ER, E, ET, OB, CH, CP, PR, LH, F, XS, XR, T, ZS, ZR, V, U,
    WG, TG, WS, WX, WR,
    loc, es, er, e2s, e2r, ws, wr, ys, yr, cs, cr, gs, gr, xs, xr, rxs, rxr, rzs, rzr, ready,
):
    p = lax.axis_index("grp")
    b = lax.axis_index("blk")
    x_lo, y = p // NY, p % NY
    x_hi, z, c = b // (2 * NZ), (b // 2) % NZ, b % 2
    x_other = x_hi ^ 1

    def at_blk(xh, zz, cc):
        return {"blk": xh * (2 * NZ) + zz * 2 + cc}

    quad = {
        k: at_blk(x_hi ^ 1 if k & 2 else x_hi, z, c ^ 1 if k & 1 else c) for k in (1, 2, 3)
    }
    y_dev = ({"grp": x_lo * NY + (y + 1) % NY}, {"grp": x_lo * NY + (y + NY - 1) % NY})
    x_dev = {"grp": (x_lo ^ 1) * NY + y}
    started = []

    def rcopy(src, dst, s, r, dev):
        return pltpu.make_async_remote_copy(
            src_ref=src, dst_ref=dst, send_sem=s, recv_sem=r, device_id=dev, device_id_type=MESH
        )

    def send(src, dst, s, r, dev, when=None):
        copy = rcopy(src, dst, s, r, dev)
        if when is None:
            copy.start()
        else:
            pl.when(when)(lambda: copy.start())
        started.append((when, copy))

    def arrived(ref, s, r, when=None):
        copy = rcopy(ref, ref, s, r, quad[1])
        if when is None:
            copy.wait_recv()
        else:
            pl.when(when)(lambda: copy.wait_recv())

    local = [
        pltpu.make_async_copy(walkers, XW, loc.at[0]),
        pltpu.make_async_copy(fields, FI, loc.at[1]),
        pltpu.make_async_copy(field_diag, FD, loc.at[2]),
        pltpu.make_async_copy(one_body, OB, loc.at[3]),
        pltpu.make_async_copy(chol, CH.at[0], loc.at[4]),
        pltpu.make_async_copy(weights, WG, loc.at[5]),
        pltpu.make_async_copy(target, TG, loc.at[6]),
    ]
    for copy in local:
        copy.start()

    def say(sem, zz, k):
        pl.semaphore_signal(sem, inc=1, device_id=at_blk(x_hi, zz, c ^ k), device_id_type=MESH)

    barrier = pltpu.get_barrier_semaphore()
    always = list(quad.values()) + list(y_dev) + [x_dev]
    for dev in always:
        pl.semaphore_signal(barrier, inc=1, device_id=dev, device_id_type=MESH)
    for zz in range(1, NZ):

        @pl.when(zz > z)
        def _(zz=zz):
            say(barrier, zz, 0)
            say(barrier, zz, 1)

    pl.semaphore_wait(barrier, len(always) + 2 * z)
    for zz in range(NZ - 1):

        @pl.when(zz < z)
        def _(zz=zz):
            say(ready.at[z, 0], zz, 0)
            say(ready.at[z, 1], zz, 1)

    local[0].wait()
    low = lax.broadcasted_iota(jnp.int32, (SLOTS, NORB), 0) < HALF
    for r in range(0, ROWS, 2):
        one, two = XW[r].astype(F32), XW[r + 1].astype(F32)
        first = jnp.where(low, one, pltpu.roll(two, HALF, 0))
        second = jnp.where(low, pltpu.roll(one, HALF, 0), two)
        WP[0, r // 2] = first.astype(BF16)
        WP[1, r // 2] = second.astype(BF16)
        GP[x_hi, z, c, r // 2] = jnp.where(c == 0, first, second).astype(BF16)

    def spread(zz, when):
        for k in range(2):
            send(
                WP.at[c ^ k], GP.at[x_hi, z, c], gs.at[zz, k], gr.at[z, k],
                at_blk(x_hi, zz, c ^ k), when,
            )

    send(WP.at[c], GP.at[x_hi, z, c], xs.at[z, 0], xr.at[z, 0], quad[2])
    for d in RING[1:]:
        spread((z + d) % NZ, (z + d) % NZ < z)
    send(WP.at[c ^ 1], GP.at[x_hi, z, c], gs.at[z, 1], gr.at[z, 1], quad[1])

    local[1].wait()
    local[2].wait()
    part = FI[:, 0:1] * FD[0:1, :]
    for k in range(1, VEC):
        part += FI[:, k : k + 1] * FD[k : k + 1, :]
    EP[0] = part[:HALF]
    EP[1] = part[HALF:]
    for k in (3, 2, 1):
        send(EP.at[c ^ 1 if k & 1 else c], ER.at[k - 1], es.at[k - 1], er.at[k - 1], quad[k])

    local[5].wait()
    local[6].wait()
    live = jnp.where(TG[...] < LIVE, WG[...], jnp.float32(0.0))
    same = lax.broadcasted_iota(jnp.int32, (SLOTS, SLOTS), 0) == lax.broadcasted_iota(
        jnp.int32, (SLOTS, SLOTS), 1
    )
    mine = jnp.sum(
        jnp.where(same, jnp.broadcast_to(live, (SLOTS, SLOTS)), 0.0), axis=1, keepdims=True
    )
    WS[...] = jnp.broadcast_to(jnp.sum(live, axis=1, keepdims=True), (8, 128))
    send(chol, CH.at[1], cs, cr, quad[1])
    send(WS, WX, ws, wr, x_dev)

    def rotate(part, t):
        rows = pl.ds(t * 3 * NOCC, 3 * NOCC)
        flat = CH.at[part].reshape(VEC * NOCC, NORB)
        CP[part, rows, :] = lax.dot_general(
            flat[rows, :], OB[...], (((1,), (1,)), ((), ())), preferred_element_type=F32
        ).astype(BF16)

    def onward(zz):
        for k in range(2):
            when = None if k else z != zz
            ref = GP.at[x_hi, zz, c ^ k]
            arrived(ref, gs.at[zz, k], gr.at[zz, k], when)
            send(ref, ref, xs.at[zz, k], xr.at[zz, k], quad[2], when)

    def weigh(step):
        for way, steps in enumerate((4, 3)):
            if step > 1 and step - 1 <= steps:
                ref = WR.at[(y + NY - step + 1) % NY if way == 0 else (y + step - 1) % NY]
                arrived(ref, ys.at[way, step - 2], yr.at[way, step - 2])
            if step <= steps:
                ref = WR.at[(y + NY - step + 1) % NY if way == 0 else (y + step - 1) % NY]
                send(ref, ref, ys.at[way, step - 1], yr.at[way, step - 1], y_dev[way])

    for j in range(1, NZ):
        later = z + j < NZ
        zz = jnp.minimum(z + j, NZ - 1)

        @pl.when(later)
        def _(zz=zz):
            pl.semaphore_wait(ready.at[zz, 0], 1)
            pl.semaphore_wait(ready.at[zz, 1], 1)

        spread(zz, later)
        if j == 1:
            local[3].wait()
            local[4].wait()
        if j == 3:
            for k in range(3):
                arrived(ER.at[k], es.at[k], er.at[k])
            E[z] = (EP[c] + ER[1]) + (ER[0] + ER[2])
            for d in RING[1:]:
                other = (z + d) % NZ
                send(
                    E.at[z], E.at[z], e2s.at[other], e2r.at[z],
                    at_blk(x_hi, other, c), other < z + j + 1,
                )
        if j > 3:
            send(E.at[z], E.at[z], e2s.at[zz], e2r.at[z], at_blk(x_hi, zz, c), later)
            onward(j - 4)
        if j == 5:
            arrived(CH.at[1], cs, cr)
        rotate(j // 5, (j - 1) % 4)
    rotate(1, 3)
    arrived(WX, ws, wr)
    WR[y] = WS[...] + WX[...]
    weigh(1)
    for zz in range(4, NZ):
        onward(zz)
    for zz in range(NZ):
        arrived(E.at[zz], e2s.at[zz], e2r.at[zz], z != zz)
    total = E[0]
    for i in range(1, NZ):
        total += E[i]
    grown = jnp.exp(total)
    ET[0:HALF, :] = grown
    ET[HALF:SLOTS, :] = grown

    def scale(xh, zz, k):
        base = (xh * 2 * NZ + zz * 2 + (c ^ k)) * ROWS * HALF
        for h in range(2):
            rows = GP[xh, zz, c ^ k, h].astype(F32) * ET[...]
            at = pl.ds(pl.multiple_of(base + h * SLOTS, SLOTS), SLOTS)
            for n in range(LANES):
                S[n, at, :] = rows[:, n * 128 : (n + 1) * 128]

    def gathered(xh):
        for w in range(HALF):
            at = pl.ds(pl.multiple_of(w * NOCC + xh * (NOCC // 2), NOCC // 2), NOCC // 2)
            for n in range(LANES):
                PR[at, n * 128 : (n + 1) * 128] = S[
                    n, pl.ds(xh * (NOCC * HALF // 2) + w, NOCC // 2, stride=HALF), :
                ].astype(BF16)

    for zz in range(NZ):
        for k in range(2):
            scale(x_hi, zz, k)
    gathered(x_hi)
    for zz in range(NZ):
        for k in range(2):
            arrived(GP.at[x_other, zz, c ^ k], xs.at[zz, k], xr.at[zz, k])
            scale(x_other, zz, k)
    gathered(x_other)
    weigh(2)

    vectors = CH.reshape(2 * VEC * NOCC, NORB)
    rotated = CP.reshape(2 * VEC * NOCC, NORB)

    def compute(pair):
        base = pair * 2 * NOCC
        for t in range(2 * VEC // TV):
            res = lax.dot_general(
                rotated[t * TV * NOCC : (t + 1) * TV * NOCC, :], PR[base : base + 2 * NOCC, :],
                (((1,), (1,)), ((), ())), preferred_element_type=F32,
            ).astype(BF16)
            for g in range(TV):
                for w in range(2):
                    LH[w * NOCC : (w + 1) * NOCC, (t * TV + g) * NOCC : (t * TV + g + 1) * NOCC] = res[
                        g * NOCC : (g + 1) * NOCC, w * NOCC : (w + 1) * NOCC
                    ]
        for n in range(NORB // 256):
            F[base : base + 2 * NOCC, n * 256 : (n + 1) * 256] = jnp.dot(
                LH[...], vectors[:, n * 256 : (n + 1) * 256], preferred_element_type=F32
            )

    def rows_of(pair, w, xh, zp):
        start = (pair * 2 + w) * NOCC + xh * (NOCC // 2) + zp * ZROWS
        return F[pl.ds(pl.multiple_of(start, ZROWS), ZROWS), :]

    def cross(pair, zp):
        for w in range(2):
            XS[pair, zp, w] = rows_of(pair, w, x_other, zp).astype(BF16)
        send(XS.at[pair, zp], XR.at[pair, zp], rxs.at[pair, zp], rxr.at[pair, zp], quad[2])

    def deliver(pair, zp):
        arrived(XR.at[pair, zp], rxs.at[pair, zp], rxr.at[pair, zp])
        for w in range(2):
            rows = rows_of(pair, w, x_hi, zp) + XR[pair, zp, w].astype(F32)
            for n in range(LANES):
                T[pair, zp, n, pl.ds(w, ZROWS, stride=2), :] = rows[:, n * 128 : (n + 1) * 128]
        for h in range(2):
            zz = zp * 2 + h
            for cc in range(2):
                for n in range(LANES):
                    ZS[pair, zz, cc, :, n * 128 : (n + 1) * 128] = T[
                        pair, zp, n, (h * 2 + cc) * 8 : (h * 2 + cc) * 8 + 8, :
                    ].astype(BF16)
        for h in range(2):
            zz = zp * 2 + h
            for kc in range(2):
                send(
                    ZS.at[pair, zz, c ^ kc], ZR.at[pair, z, c],
                    rzs.at[pair, zz, kc], rzr.at[pair, z, kc],
                    at_blk(x_hi, zz, c ^ kc), None if kc else z != zz,
                )

    def collect(pair):
        ZR[pair, z, c] = ZS[pair, z, c]
        for kc in range(2):
            acc = None
            for zs in range(NZ):
                ref = ZR.at[pair, zs, c ^ kc]
                arrived(ref, rzs.at[pair, zs, kc], rzr.at[pair, zs, kc], None if kc else z != zs)
                rows = ref[...].astype(F32)
                acc = rows if acc is None else acc + rows
            at = pl.ds(pl.multiple_of((c ^ kc) * 16 + pair * 8, 8), 8)
            for n in range(LANES):
                V[n, at, :] = acc[:, n * 128 : (n + 1) * 128]

    compute(0)
    for zp in range(NZ // 2):
        cross(0, zp)
    weigh(3)
    compute(1)
    for zp in range(NZ // 2):
        cross(1, zp)
    for pair in range(2):
        for zp in range(NZ // 2):
            deliver(pair, zp)
        weigh(4 + pair)
    total = WR[0]
    for i in range(1, NY):
        total += WR[i]
    factor = jnp.broadcast_to(mine * LIVE, (8, 128)) / total

    for pair in range(2):
        collect(pair)
    for slot in range(SLOTS):
        for n in range(LANES):
            U[n, pl.ds(slot, ROWS, stride=SLOTS), :] = V[
                n, pl.ds((slot // 2) * 8 + slot % 2, ROWS, stride=2), :
            ]
    for r in range(ROWS):
        for n in range(LANES):
            raw = U[n, r * SLOTS : (r + 1) * SLOTS, :].astype(BF16).astype(F32)
            out[r, :, n * 128 : (n + 1) * 128] = (raw * factor).astype(BF16)

    for when, copy in started:
        if when is None:
            copy.wait_send()
        else:
            pl.when(when)(lambda copy=copy: copy.wait_send())


def body(walkers, one_body, fields, field_diag, chol, weights, target):
    vmem, sem = pltpu.VMEM, pltpu.SemaphoreType.DMA
    any_ = pl.BlockSpec(memory_space=pl.ANY)
    return pl.pallas_call(
        kernel,
        out_shape=pltpu.VMEM((ROWS, SLOTS, NORB), BF16),
        in_specs=[any_] * 7,
        out_specs=pl.BlockSpec(memory_space=pltpu.VMEM),
        scratch_shapes=[
            vmem((ROWS, SLOTS, NORB), BF16),
            vmem((2, 2, SLOTS, NORB), BF16),
            vmem((2, NZ, 2, 2, SLOTS, NORB), BF16),
            vmem((LANES, NOCC * HALF, 128), F32),
            vmem((SLOTS, VEC), F32),
            vmem((VEC, NORB), F32),
            vmem((2, HALF, NORB), F32),
            vmem((3, HALF, NORB), F32),
            vmem((NZ, HALF, NORB), F32),
            vmem((SLOTS, NORB), F32),
            vmem((NORB, NORB), BF16),
            vmem((2, VEC, NOCC, NORB), BF16),
            vmem((2, VEC * NOCC, NORB), BF16),
            vmem((HALF * NOCC, NORB), BF16),
            vmem((2 * NOCC, 2 * VEC * NOCC), BF16),
            vmem((HALF * NOCC, NORB), F32),
            vmem((2, 4, 2, ZROWS, NORB), BF16),
            vmem((2, 4, 2, ZROWS, NORB), BF16),
            vmem((2, 4, LANES, 2 * ZROWS, 128), F32),
            vmem((2, NZ, 2, 8, NORB), BF16),
            vmem((2, NZ, 2, 8, NORB), BF16),
            vmem((LANES, 32, 128), F32),
            vmem((LANES, 32, 128), F32),
            vmem((1, SLOTS), F32),
            vmem((1, SLOTS), jnp.int32),
            vmem((8, 128), F32),
            vmem((8, 128), F32),
            vmem((NY, 8, 128), F32),
            sem((7,)),
            sem((3,)), sem((3,)),
            sem((NZ,)), sem((NZ,)),
            sem, sem,
            sem((2, 4)), sem((2, 4)),
            sem, sem,
            sem((NZ, 2)), sem((NZ, 2)),
            sem((NZ, 2)), sem((NZ, 2)),
            sem((2, 4)), sem((2, 4)),
            sem((2, NZ, 2)), sem((2, NZ, 2)),
            pltpu.SemaphoreType.REGULAR((NZ, 2)),
        ],
        compiler_params=pltpu.CompilerParams(
            collective_id=0, has_side_effects=True, vmem_limit_bytes=56 * 1024 * 1024
        ),
    )(
        walkers, one_body, fields, field_diag, chol,
        weights.reshape(1, SLOTS), target.reshape(1, SLOTS),
    )


def solution(mesh):
    in_specs = (
        P("blk", "grp", None),
        P(),
        P("grp", "blk"),
        P("blk", None),
        P("blk", None, None),
        P("grp"),
        P("grp"),
    )
    out_specs = P("blk", "grp", None)
    return jax.shard_map(body, mesh=mesh, in_specs=in_specs, out_specs=out_specs, check_vma=False)
```

```python
import jax
import jax.numpy as jnp
from jax import lax
from jax.experimental import pallas as pl
from jax.experimental.pallas import tpu as pltpu
from jax.sharding import PartitionSpec as P

MESH = pl.DeviceIdType.MESH
F32 = jnp.float32
BF16 = jnp.bfloat16

NZ = 8
NY = 8
SLOTS = 8
HALF = SLOTS // 2
ROWS = 4
QUAD = 4
ZROWS = QUAD * ROWS
NOCC = NZ * ZROWS
NORB = 768
LANES = NORB // 128
VEC = 12
TV = 6
LIVE = 64
ORDER = (2, 1, 3, 0)

RING = (0, 1, 7, 2, 6, 3, 5, 4)


def kernel(
    walkers, one_body, fields, field_diag, chol, weights, target, out,
    XW, WP, GP, S, FI, FD, EP, ER, E, ET, OB, CH, CP, PR, LH, F, XS, XR, T, ZS, ZR, V, U,
    WS, WX, WR,
    loc, es, er, e2s, e2r, ws, wr, ys, yr, cs, cr, gs, gr, xs, xr, rxs, rxr, rzs, rzr,
):
    p = lax.axis_index("grp")
    b = lax.axis_index("blk")
    x_lo, y = p // NY, p % NY
    x_hi, z, c = b // (2 * NZ), (b // 2) % NZ, b % 2
    x_other = x_hi ^ 1

    def at_blk(xh, zz, cc):
        return {"blk": xh * (2 * NZ) + zz * 2 + cc}

    quad = {
        k: at_blk(x_hi ^ 1 if k & 2 else x_hi, z, c ^ 1 if k & 1 else c) for k in (1, 2, 3)
    }
    column = {
        (d, k): at_blk(x_hi, (z + d) % NZ, c ^ k) for d in RING for k in range(2) if d or k
    }
    y_dev = ({"grp": x_lo * NY + (y + 1) % NY}, {"grp": x_lo * NY + (y + NY - 1) % NY})
    x_dev = {"grp": (x_lo ^ 1) * NY + y}
    started = []

    def rcopy(src, dst, s, r, dev):
        return pltpu.make_async_remote_copy(
            src_ref=src, dst_ref=dst, send_sem=s, recv_sem=r, device_id=dev, device_id_type=MESH
        )

    def send(src, dst, s, r, dev):
        copy = rcopy(src, dst, s, r, dev)
        copy.start()
        started.append(copy)

    def arrived(ref, s, r):
        rcopy(ref, ref, s, r, quad[1]).wait_recv()

    local = [
        pltpu.make_async_copy(walkers, XW, loc.at[0]),
        pltpu.make_async_copy(fields, FI, loc.at[1]),
        pltpu.make_async_copy(field_diag, FD, loc.at[2]),
        pltpu.make_async_copy(one_body, OB, loc.at[3]),
        pltpu.make_async_copy(chol, CH.at[0], loc.at[4]),
    ]
    for copy in local:
        copy.start()

    barrier = pltpu.get_barrier_semaphore()
    partners = list(column.values()) + [quad[2], quad[3]] + list(y_dev) + [x_dev]
    for dev in partners:
        pl.semaphore_signal(barrier, inc=1, device_id=dev, device_id_type=MESH)

    local[0].wait()
    low = lax.broadcasted_iota(jnp.int32, (SLOTS, NORB), 0) < HALF
    for r in range(0, ROWS, 2):
        one, two = XW[r].astype(F32), XW[r + 1].astype(F32)
        first = jnp.where(low, one, pltpu.roll(two, HALF, 0))
        second = jnp.where(low, pltpu.roll(one, HALF, 0), two)
        WP[0, r // 2] = first.astype(BF16)
        WP[1, r // 2] = second.astype(BF16)
        GP[x_hi, z, c, r // 2] = jnp.where(c == 0, first, second).astype(BF16)

    local[1].wait()
    local[2].wait()
    part = FI[:, 0:1] * FD[0:1, :]
    for k in range(1, VEC):
        part += FI[:, k : k + 1] * FD[k : k + 1, :]
    EP[0] = part[:HALF]
    EP[1] = part[HALF:]

    own = jnp.float32(0.0)
    for s in range(SLOTS):
        own = own + jnp.where(target[s] < LIVE, weights[s], jnp.float32(0.0))
    WS[...] = jnp.full((8, 128), own, F32)

    pl.semaphore_wait(barrier, len(partners))

    for k in (3, 2, 1):
        send(EP.at[c ^ 1 if k & 1 else c], ER.at[k - 1], es.at[k - 1], er.at[k - 1], quad[k])
    send(WP.at[c], GP.at[x_hi, z, c], xs.at[0, 0], xr.at[0, 0], quad[2])

    def spread(d):
        for k in range(2):
            if d or k:
                send(WP.at[c ^ k], GP.at[x_hi, z, c], gs.at[d, k], gr.at[d, k], column[d, k])

    for d in RING[:5]:
        spread(d)
    send(WS, WX, ws, wr, x_dev)
    send(chol, CH.at[1], cs, cr, quad[1])

    for k in range(3):
        arrived(ER.at[k], es.at[k], er.at[k])
    E[z] = (EP[c] + ER[1]) + (ER[0] + ER[2])
    for d in RING[1:]:
        send(E.at[z], E.at[z], e2s.at[d - 1], e2r.at[d - 1], column[d, 0])
    for d in RING[5:]:
        spread(d)

    def rotate(part, t):
        rows = pl.ds(t * 3 * NOCC, 3 * NOCC)
        flat = CH.at[part].reshape(VEC * NOCC, NORB)
        CP[part, rows, :] = lax.dot_general(
            flat[rows, :], OB[...], (((1,), (1,)), ((), ())), preferred_element_type=F32
        ).astype(BF16)

    def onward(d):
        for k in range(2):
            if d or k:
                ref = GP.at[x_hi, (z + NZ - d) % NZ, c ^ k]
                arrived(ref, gs.at[d, k], gr.at[d, k])
                send(ref, ref, xs.at[d, k], xr.at[d, k], quad[2])

    def weigh(step):
        for way, steps in enumerate((4, 3)):
            if step > 1 and step - 1 <= steps:
                ref = WR.at[(y + NY - step + 1) % NY if way == 0 else (y + step - 1) % NY]
                arrived(ref, ys.at[way, step - 2], yr.at[way, step - 2])
            if step <= steps:
                ref = WR.at[(y + NY - step + 1) % NY if way == 0 else (y + step - 1) % NY]
                send(ref, ref, ys.at[way, step - 1], yr.at[way, step - 1], y_dev[way])

    local[3].wait()
    local[4].wait()
    onward(0)
    rotate(0, 0)
    onward(1)
    onward(7)
    rotate(0, 1)
    onward(2)
    onward(6)
    arrived(WX, ws, wr)
    WR[y] = WS[...] + WX[...]
    weigh(1)
    rotate(0, 2)
    onward(3)
    onward(5)
    rotate(0, 3)
    onward(4)
    weigh(2)
    arrived(CH.at[1], cs, cr)

    for d in RING[1:]:
        arrived(E.at[(z + NZ - d) % NZ], e2s.at[d - 1], e2r.at[d - 1])
    total = E[0]
    for i in range(1, NZ):
        total += E[i]
    grown = jnp.exp(total)
    ET[0:HALF, :] = grown
    ET[HALF:SLOTS, :] = grown

    def scale(xh, d, k):
        zz = (z + NZ - d) % NZ
        base = (xh * 2 * NZ + zz * 2 + (c ^ k)) * ROWS * HALF
        for h in range(2):
            rows = GP[xh, zz, c ^ k, h].astype(F32) * ET[...]
            at = pl.ds(pl.multiple_of(base + h * SLOTS, SLOTS), SLOTS)
            for n in range(LANES):
                S[n, at, :] = rows[:, n * 128 : (n + 1) * 128]

    for i, d in enumerate(RING):
        for k in range(2):
            scale(x_hi, d, k)
        if i % 2:
            rotate(1, i // 2)
    for d in RING:
        for k in range(2):
            arrived(GP.at[x_other, (z + NZ - d) % NZ, c ^ k], xs.at[d, k], xr.at[d, k])
            scale(x_other, d, k)
    weigh(3)
    for w in range(HALF):
        for n in range(LANES):
            PR[w * NOCC : (w + 1) * NOCC, n * 128 : (n + 1) * 128] = S[
                n, pl.ds(w, NOCC, stride=HALF), :
            ].astype(BF16)

    vectors = CH.reshape(2 * VEC * NOCC, NORB)
    rotated = CP.reshape(2 * VEC * NOCC, NORB)

    def compute(pair):
        base = pair * 2 * NOCC
        for t in range(2 * VEC // TV):
            res = lax.dot_general(
                rotated[t * TV * NOCC : (t + 1) * TV * NOCC, :], PR[base : base + 2 * NOCC, :],
                (((1,), (1,)), ((), ())), preferred_element_type=F32,
            ).astype(BF16)
            for g in range(TV):
                for w in range(2):
                    LH[w * NOCC : (w + 1) * NOCC, (t * TV + g) * NOCC : (t * TV + g + 1) * NOCC] = res[
                        g * NOCC : (g + 1) * NOCC, w * NOCC : (w + 1) * NOCC
                    ]
        for n in range(NORB // 256):
            F[base : base + 2 * NOCC, n * 256 : (n + 1) * 256] = jnp.dot(
                LH[...], vectors[:, n * 256 : (n + 1) * 256], preferred_element_type=F32
            )

    def near(k):
        return (z // 2 + k) % (NZ // 2)

    def rows_of(pair, w, xh, zp):
        start = (pair * 2 + w) * NOCC + xh * (NOCC // 2) + zp * ZROWS
        return F[pl.ds(pl.multiple_of(start, ZROWS), ZROWS), :]

    def cross(pair, k):
        for w in range(2):
            XS[pair, k, w] = rows_of(pair, w, x_other, near(k)).astype(BF16)
        send(XS.at[pair, k], XR.at[pair, k], rxs.at[pair, k], rxr.at[pair, k], quad[2])

    def deliver(pair, k):
        arrived(XR.at[pair, k], rxs.at[pair, k], rxr.at[pair, k])
        for w in range(2):
            rows = rows_of(pair, w, x_hi, near(k)) + XR[pair, k, w].astype(F32)
            for n in range(LANES):
                T[pair, k, n, pl.ds(w, ZROWS, stride=2), :] = rows[:, n * 128 : (n + 1) * 128]
        for h in range(2):
            for cc in range(2):
                for n in range(LANES):
                    ZS[pair, k, h, cc, :, n * 128 : (n + 1) * 128] = T[
                        pair, k, n, (h * 2 + cc) * 8 : (h * 2 + cc) * 8 + 8, :
                    ].astype(BF16)
        for t in range(2):
            h = (z % 2) ^ t
            for kc in range(2):
                if k or t or kc:
                    send(
                        ZS.at[pair, k, h, c ^ kc], ZR.at[pair, z, c],
                        rzs.at[pair, k, t, kc], rzr.at[pair, k, t, kc],
                        at_blk(x_hi, near(k) * 2 + h, c ^ kc),
                    )

    def collect(pair):
        for kc in range(2):
            acc = None
            for k in ORDER:
                for t in range(2):
                    zs = ((z // 2 + NZ // 2 - k) % (NZ // 2)) * 2 + ((z % 2) ^ t)
                    if k or t or kc:
                        ref = ZR.at[pair, zs, c ^ kc]
                        arrived(ref, rzs.at[pair, k, t, kc], rzr.at[pair, k, t, kc])
                        rows = ref[...].astype(F32)
                    else:
                        rows = ZS[pair, 0, z % 2, c].astype(F32)
                    acc = rows if acc is None else acc + rows
            at = pl.ds(pl.multiple_of((c ^ kc) * 16 + pair * 8, 8), 8)
            for n in range(LANES):
                V[n, at, :] = acc[:, n * 128 : (n + 1) * 128]

    compute(0)
    for k in ORDER:
        cross(0, k)
    compute(1)
    for k in ORDER:
        cross(1, k)
    weigh(4)
    for pair in range(2):
        for k in ORDER:
            deliver(pair, k)
    weigh(5)
    total = WR[0]
    for i in range(1, NY):
        total += WR[i]
    row = lax.broadcasted_iota(jnp.int32, (8, 128), 0)
    factor = jnp.zeros((8, 128), F32)
    for s in range(SLOTS):
        mine = jnp.where(target[s] < LIVE, weights[s] * LIVE, jnp.float32(0.0))
        factor = jnp.where(row == s, mine, factor)
    factor = factor / total

    for pair in range(2):
        collect(pair)
    for slot in range(SLOTS):
        for n in range(LANES):
            U[n, pl.ds(slot, ROWS, stride=SLOTS), :] = V[
                n, pl.ds((slot // 2) * 8 + slot % 2, ROWS, stride=2), :
            ]
    for r in range(ROWS):
        for n in range(LANES):
            raw = U[n, r * SLOTS : (r + 1) * SLOTS, :].astype(BF16).astype(F32)
            out[r, :, n * 128 : (n + 1) * 128] = (raw * factor).astype(BF16)

    for copy in started:
        copy.wait_send()


def body(walkers, one_body, fields, field_diag, chol, weights, target):
    vmem, sem = pltpu.VMEM, pltpu.SemaphoreType.DMA
    any_, smem = pl.BlockSpec(memory_space=pl.ANY), pl.BlockSpec(memory_space=pltpu.SMEM)
    return pl.pallas_call(
        kernel,
        out_shape=pltpu.VMEM((ROWS, SLOTS, NORB), BF16),
        in_specs=[any_] * 5 + [smem] * 2,
        out_specs=pl.BlockSpec(memory_space=pltpu.VMEM),
        scratch_shapes=[
            vmem((ROWS, SLOTS, NORB), BF16),
            vmem((2, 2, SLOTS, NORB), BF16),
            vmem((2, NZ, 2, 2, SLOTS, NORB), BF16),
            vmem((LANES, NOCC * HALF, 128), F32),
            vmem((SLOTS, VEC), F32),
            vmem((VEC, NORB), F32),
            vmem((2, HALF, NORB), F32),
            vmem((3, HALF, NORB), F32),
            vmem((NZ, HALF, NORB), F32),
            vmem((SLOTS, NORB), F32),
            vmem((NORB, NORB), BF16),
            vmem((2, VEC, NOCC, NORB), BF16),
            vmem((2, VEC * NOCC, NORB), BF16),
            vmem((HALF * NOCC, NORB), BF16),
            vmem((2 * NOCC, 2 * VEC * NOCC), BF16),
            vmem((HALF * NOCC, NORB), F32),
            vmem((2, 4, 2, ZROWS, NORB), BF16),
            vmem((2, 4, 2, ZROWS, NORB), BF16),
            vmem((2, 4, LANES, 2 * ZROWS, 128), F32),
            vmem((2, 4, 2, 2, 8, NORB), BF16),
            vmem((2, NZ, 2, 8, NORB), BF16),
            vmem((LANES, 32, 128), F32),
            vmem((LANES, 32, 128), F32),
            vmem((8, 128), F32),
            vmem((8, 128), F32),
            vmem((NY, 8, 128), F32),
            sem((5,)),
            sem((3,)), sem((3,)),
            sem((7,)), sem((7,)),
            sem, sem,
            sem((2, 4)), sem((2, 4)),
            sem, sem,
            sem((NZ, 2)), sem((NZ, 2)),
            sem((NZ, 2)), sem((NZ, 2)),
            sem((2, 4)), sem((2, 4)),
            sem((2, 4, 2, 2)), sem((2, 4, 2, 2)),
        ],
        compiler_params=pltpu.CompilerParams(
            collective_id=0, has_side_effects=True, vmem_limit_bytes=56 * 1024 * 1024
        ),
    )(walkers, one_body, fields, field_diag, chol, weights, target)


def solution(mesh):
    in_specs = (
        P("blk", "grp", None),
        P(),
        P("grp", "blk"),
        P("blk", None),
        P("blk", None, None),
        P("grp"),
        P("grp"),
    )
    out_specs = P("blk", "grp", None)
    return jax.shard_map(body, mesh=mesh, in_specs=in_specs, out_specs=out_specs, check_vma=False)
```

```python
import jax
import jax.numpy as jnp
from jax import lax
from jax.experimental import pallas as pl
from jax.experimental.pallas import tpu as pltpu
from jax.sharding import PartitionSpec as P

MESH = pl.DeviceIdType.MESH
F32 = jnp.float32
BF16 = jnp.bfloat16

NZ = 8
NY = 8
SLOTS = 8
HALF = SLOTS // 2
ROWS = 4
QUAD = 4
ZROWS = QUAD * ROWS
NOCC = NZ * ZROWS
NORB = 768
LANES = NORB // 128
VEC = 12
TV = 6
LIVE = 64
ORDER = (2, 1, 3, 0)

RING = (0, 1, 7, 2, 6, 3, 5, 4)


def kernel(
    walkers, one_body, fields, field_diag, chol, weights, target, out,
    XW, WP, GP, S, FI, FD, EP, ER, E, ET, OB, CH, CP, PR, LH, F, XS, XR, T, ZS, ZR, V, U,
    WG, TG, WS, WX, WR,
    loc, es, er, e2s, e2r, ws, wr, ys, yr, cs, cr, gs, gr, xs, xr, rxs, rxr, rzs, rzr, fs, fr,
):
    p = lax.axis_index("grp")
    b = lax.axis_index("blk")
    x_lo, y = p // NY, p % NY
    x_hi, z, c = b // (2 * NZ), (b // 2) % NZ, b % 2
    x_other = x_hi ^ 1

    def at_blk(xh, zz, cc):
        return {"blk": xh * (2 * NZ) + zz * 2 + cc}

    quad = {
        k: at_blk(x_hi ^ 1 if k & 2 else x_hi, z, c ^ 1 if k & 1 else c) for k in (1, 2, 3)
    }
    column = {
        (d, k): at_blk(x_hi, (z + d) % NZ, c ^ k) for d in RING for k in range(2) if d or k
    }
    y_dev = ({"grp": x_lo * NY + (y + 1) % NY}, {"grp": x_lo * NY + (y + NY - 1) % NY})
    x_dev = {"grp": (x_lo ^ 1) * NY + y}
    started = []

    def rcopy(src, dst, s, r, dev):
        return pltpu.make_async_remote_copy(
            src_ref=src, dst_ref=dst, send_sem=s, recv_sem=r, device_id=dev, device_id_type=MESH
        )

    def send(src, dst, s, r, dev):
        copy = rcopy(src, dst, s, r, dev)
        copy.start()
        started.append(copy)

    def arrived(ref, s, r):
        rcopy(ref, ref, s, r, quad[1]).wait_recv()

    local = [
        pltpu.make_async_copy(walkers, XW, loc.at[0]),
        pltpu.make_async_copy(fields, FI, loc.at[1]),
        pltpu.make_async_copy(field_diag, FD, loc.at[2]),
        pltpu.make_async_copy(one_body, OB, loc.at[3]),
        pltpu.make_async_copy(chol, CH.at[0], loc.at[4]),
        pltpu.make_async_copy(weights, WG, loc.at[5]),
        pltpu.make_async_copy(target, TG, loc.at[6]),
    ]
    for copy in local:
        copy.start()

    barrier = pltpu.get_barrier_semaphore()
    partners = list(column.values()) + [quad[2], quad[3]] + list(y_dev) + [x_dev]
    for dev in partners:
        pl.semaphore_signal(barrier, inc=1, device_id=dev, device_id_type=MESH)

    local[0].wait()
    low = lax.broadcasted_iota(jnp.int32, (SLOTS, NORB), 0) < HALF
    for r in range(0, ROWS, 2):
        one, two = XW[r].astype(F32), XW[r + 1].astype(F32)
        first = jnp.where(low, one, pltpu.roll(two, HALF, 0))
        second = jnp.where(low, pltpu.roll(one, HALF, 0), two)
        WP[0, r // 2] = first.astype(BF16)
        WP[1, r // 2] = second.astype(BF16)
        GP[x_hi, z, c, r // 2] = jnp.where(c == 0, first, second).astype(BF16)

    local[1].wait()
    local[2].wait()
    part = FI[:, 0:1] * FD[0:1, :]
    for k in range(1, VEC):
        part += FI[:, k : k + 1] * FD[k : k + 1, :]
    EP[0] = part[:HALF]
    EP[1] = part[HALF:]

    local[5].wait()
    local[6].wait()
    live = jnp.where(TG[...] < LIVE, WG[...], jnp.float32(0.0))
    same = lax.broadcasted_iota(jnp.int32, (SLOTS, SLOTS), 0) == lax.broadcasted_iota(
        jnp.int32, (SLOTS, SLOTS), 1
    )
    mine = jnp.sum(
        jnp.where(same, jnp.broadcast_to(live, (SLOTS, SLOTS)), 0.0), axis=1, keepdims=True
    )
    WS[...] = jnp.broadcast_to(jnp.sum(live, axis=1, keepdims=True), (8, 128))

    pl.semaphore_wait(barrier, len(partners))

    for k in (3, 2, 1):
        send(EP.at[c ^ 1 if k & 1 else c], ER.at[k - 1], es.at[k - 1], er.at[k - 1], quad[k])
    send(WP.at[c], GP.at[x_hi, z, c], xs.at[0, 0], xr.at[0, 0], quad[2])

    def spread(d):
        for k in range(2):
            if d or k:
                send(WP.at[c ^ k], GP.at[x_hi, z, c], gs.at[d, k], gr.at[d, k], column[d, k])

    for d in RING[:5]:
        spread(d)
    send(chol, CH.at[1], cs, cr, quad[1])
    send(WS, WX, ws, wr, x_dev)

    for k in range(3):
        arrived(ER.at[k], es.at[k], er.at[k])
    E[z] = (EP[c] + ER[1]) + (ER[0] + ER[2])
    for d in RING[1:]:
        send(E.at[z], E.at[z], e2s.at[d - 1], e2r.at[d - 1], column[d, 0])

    def rotate(part, t):
        rows = pl.ds(t * 3 * NOCC, 3 * NOCC)
        flat = CH.at[part].reshape(VEC * NOCC, NORB)
        CP[part, rows, :] = lax.dot_general(
            flat[rows, :], OB[...], (((1,), (1,)), ((), ())), preferred_element_type=F32
        ).astype(BF16)

    def onward(d):
        for k in range(2):
            if d or k:
                ref = GP.at[x_hi, (z + NZ - d) % NZ, c ^ k]
                arrived(ref, gs.at[d, k], gr.at[d, k])
                send(ref, ref, xs.at[d, k], xr.at[d, k], quad[2])

    def weigh(step):
        for way, steps in enumerate((4, 3)):
            if step > 1 and step - 1 <= steps:
                ref = WR.at[(y + NY - step + 1) % NY if way == 0 else (y + step - 1) % NY]
                arrived(ref, ys.at[way, step - 2], yr.at[way, step - 2])
            if step <= steps:
                ref = WR.at[(y + NY - step + 1) % NY if way == 0 else (y + step - 1) % NY]
                send(ref, ref, ys.at[way, step - 1], yr.at[way, step - 1], y_dev[way])

    def crossed(d, k):
        ref = GP.at[x_other, (z + NZ - d) % NZ, c ^ k]
        if d == 4:
            arrived(ref, fs.at[k], fr.at[k])
        else:
            arrived(ref, xs.at[d, k], xr.at[d, k])

    onward(0)
    spread(3)
    spread(5)
    local[3].wait()
    local[4].wait()
    onward(1)
    onward(7)
    spread(4)
    for k in range(2):
        crossed(0, k)
        ref = GP.at[x_other, z, c ^ k]
        send(ref, ref, fs.at[k], fr.at[k], column[4, 0])
    rotate(0, 0)
    onward(2)
    onward(6)
    arrived(WX, ws, wr)
    WR[y] = WS[...] + WX[...]
    weigh(1)
    rotate(0, 1)
    rotate(0, 2)
    onward(3)
    onward(5)
    for k in range(2):
        arrived(GP.at[x_hi, (z + 4) % NZ, c ^ k], gs.at[4, k], gr.at[4, k])
    rotate(0, 3)
    weigh(2)
    arrived(CH.at[1], cs, cr)

    for d in RING[1:]:
        arrived(E.at[(z + NZ - d) % NZ], e2s.at[d - 1], e2r.at[d - 1])
    total = E[0]
    for i in range(1, NZ):
        total += E[i]
    grown = jnp.exp(total)
    ET[0:HALF, :] = grown
    ET[HALF:SLOTS, :] = grown

    def scale(xh, d, k):
        zz = (z + NZ - d) % NZ
        base = (xh * 2 * NZ + zz * 2 + (c ^ k)) * ROWS * HALF
        for h in range(2):
            rows = GP[xh, zz, c ^ k, h].astype(F32) * ET[...]
            at = pl.ds(pl.multiple_of(base + h * SLOTS, SLOTS), SLOTS)
            for n in range(LANES):
                S[n, at, :] = rows[:, n * 128 : (n + 1) * 128]

    def gathered(xh):
        for w in range(HALF):
            at = pl.ds(pl.multiple_of(w * NOCC + xh * (NOCC // 2), NOCC // 2), NOCC // 2)
            for n in range(LANES):
                PR[at, n * 128 : (n + 1) * 128] = S[
                    n, pl.ds(xh * (NOCC * HALF // 2) + w, NOCC // 2, stride=HALF), :
                ].astype(BF16)

    for i, d in enumerate(RING):
        for k in range(2):
            scale(x_hi, d, k)
        if i % 2:
            rotate(1, i // 2)
    gathered(x_hi)
    for d in RING:
        for k in range(2):
            if d:
                crossed(d, k)
            scale(x_other, d, k)
    gathered(x_other)
    weigh(3)

    vectors = CH.reshape(2 * VEC * NOCC, NORB)
    rotated = CP.reshape(2 * VEC * NOCC, NORB)

    def compute(pair):
        base = pair * 2 * NOCC
        for t in range(2 * VEC // TV):
            res = lax.dot_general(
                rotated[t * TV * NOCC : (t + 1) * TV * NOCC, :], PR[base : base + 2 * NOCC, :],
                (((1,), (1,)), ((), ())), preferred_element_type=F32,
            ).astype(BF16)
            for g in range(TV):
                for w in range(2):
                    LH[w * NOCC : (w + 1) * NOCC, (t * TV + g) * NOCC : (t * TV + g + 1) * NOCC] = res[
                        g * NOCC : (g + 1) * NOCC, w * NOCC : (w + 1) * NOCC
                    ]
        for n in range(NORB // 256):
            F[base : base + 2 * NOCC, n * 256 : (n + 1) * 256] = jnp.dot(
                LH[...], vectors[:, n * 256 : (n + 1) * 256], preferred_element_type=F32
            )

    def near(k):
        return (z // 2 + k) % (NZ // 2)

    def rows_of(pair, w, xh, zp):
        start = (pair * 2 + w) * NOCC + xh * (NOCC // 2) + zp * ZROWS
        return F[pl.ds(pl.multiple_of(start, ZROWS), ZROWS), :]

    def cross(pair, k):
        for w in range(2):
            XS[pair, k, w] = rows_of(pair, w, x_other, near(k)).astype(BF16)
        send(XS.at[pair, k], XR.at[pair, k], rxs.at[pair, k], rxr.at[pair, k], quad[2])

    def deliver(pair, k):
        arrived(XR.at[pair, k], rxs.at[pair, k], rxr.at[pair, k])
        for w in range(2):
            rows = rows_of(pair, w, x_hi, near(k)) + XR[pair, k, w].astype(F32)
            for n in range(LANES):
                T[pair, k, n, pl.ds(w, ZROWS, stride=2), :] = rows[:, n * 128 : (n + 1) * 128]
        for h in range(2):
            for cc in range(2):
                for n in range(LANES):
                    ZS[pair, k, h, cc, :, n * 128 : (n + 1) * 128] = T[
                        pair, k, n, (h * 2 + cc) * 8 : (h * 2 + cc) * 8 + 8, :
                    ].astype(BF16)
        for t in range(2):
            h = (z % 2) ^ t
            for kc in range(2):
                if k or t or kc:
                    send(
                        ZS.at[pair, k, h, c ^ kc], ZR.at[pair, z, c],
                        rzs.at[pair, k, t, kc], rzr.at[pair, k, t, kc],
                        at_blk(x_hi, near(k) * 2 + h, c ^ kc),
                    )

    def collect(pair):
        for kc in range(2):
            acc = None
            for k in ORDER:
                for t in range(2):
                    zs = ((z // 2 + NZ // 2 - k) % (NZ // 2)) * 2 + ((z % 2) ^ t)
                    if k or t or kc:
                        ref = ZR.at[pair, zs, c ^ kc]
                        arrived(ref, rzs.at[pair, k, t, kc], rzr.at[pair, k, t, kc])
                        rows = ref[...].astype(F32)
                    else:
                        rows = ZS[pair, 0, z % 2, c].astype(F32)
                    acc = rows if acc is None else acc + rows
            at = pl.ds(pl.multiple_of((c ^ kc) * 16 + pair * 8, 8), 8)
            for n in range(LANES):
                V[n, at, :] = acc[:, n * 128 : (n + 1) * 128]

    compute(0)
    for k in ORDER:
        cross(0, k)
    compute(1)
    for k in ORDER:
        cross(1, k)
    weigh(4)
    for pair in range(2):
        for k in ORDER:
            deliver(pair, k)
    weigh(5)
    total = WR[0]
    for i in range(1, NY):
        total += WR[i]
    factor = jnp.broadcast_to(mine * LIVE, (8, 128)) / total

    for pair in range(2):
        collect(pair)
    for slot in range(SLOTS):
        for n in range(LANES):
            U[n, pl.ds(slot, ROWS, stride=SLOTS), :] = V[
                n, pl.ds((slot // 2) * 8 + slot % 2, ROWS, stride=2), :
            ]
    for r in range(ROWS):
        for n in range(LANES):
            raw = U[n, r * SLOTS : (r + 1) * SLOTS, :].astype(BF16).astype(F32)
            out[r, :, n * 128 : (n + 1) * 128] = (raw * factor).astype(BF16)

    for copy in started:
        copy.wait_send()


def body(walkers, one_body, fields, field_diag, chol, weights, target):
    vmem, sem = pltpu.VMEM, pltpu.SemaphoreType.DMA
    any_ = pl.BlockSpec(memory_space=pl.ANY)
    return pl.pallas_call(
        kernel,
        out_shape=pltpu.VMEM((ROWS, SLOTS, NORB), BF16),
        in_specs=[any_] * 7,
        out_specs=pl.BlockSpec(memory_space=pltpu.VMEM),
        scratch_shapes=[
            vmem((ROWS, SLOTS, NORB), BF16),
            vmem((2, 2, SLOTS, NORB), BF16),
            vmem((2, NZ, 2, 2, SLOTS, NORB), BF16),
            vmem((LANES, NOCC * HALF, 128), F32),
            vmem((SLOTS, VEC), F32),
            vmem((VEC, NORB), F32),
            vmem((2, HALF, NORB), F32),
            vmem((3, HALF, NORB), F32),
            vmem((NZ, HALF, NORB), F32),
            vmem((SLOTS, NORB), F32),
            vmem((NORB, NORB), BF16),
            vmem((2, VEC, NOCC, NORB), BF16),
            vmem((2, VEC * NOCC, NORB), BF16),
            vmem((HALF * NOCC, NORB), BF16),
            vmem((2 * NOCC, 2 * VEC * NOCC), BF16),
            vmem((HALF * NOCC, NORB), F32),
            vmem((2, 4, 2, ZROWS, NORB), BF16),
            vmem((2, 4, 2, ZROWS, NORB), BF16),
            vmem((2, 4, LANES, 2 * ZROWS, 128), F32),
            vmem((2, 4, 2, 2, 8, NORB), BF16),
            vmem((2, NZ, 2, 8, NORB), BF16),
            vmem((LANES, 32, 128), F32),
            vmem((LANES, 32, 128), F32),
            vmem((1, SLOTS), F32),
            vmem((1, SLOTS), jnp.int32),
            vmem((8, 128), F32),
            vmem((8, 128), F32),
            vmem((NY, 8, 128), F32),
            sem((7,)),
            sem((3,)), sem((3,)),
            sem((7,)), sem((7,)),
            sem, sem,
            sem((2, 4)), sem((2, 4)),
            sem, sem,
            sem((NZ, 2)), sem((NZ, 2)),
            sem((NZ, 2)), sem((NZ, 2)),
            sem((2, 4)), sem((2, 4)),
            sem((2, 4, 2, 2)), sem((2, 4, 2, 2)),
            sem((2,)), sem((2,)),
        ],
        compiler_params=pltpu.CompilerParams(
            collective_id=0, has_side_effects=True, vmem_limit_bytes=56 * 1024 * 1024
        ),
    )(
        walkers, one_body, fields, field_diag, chol,
        weights.reshape(1, SLOTS), target.reshape(1, SLOTS),
    )


def solution(mesh):
    in_specs = (
        P("blk", "grp", None),
        P(),
        P("grp", "blk"),
        P("blk", None),
        P("blk", None, None),
        P("grp"),
        P("grp"),
    )
    out_specs = P("blk", "grp", None)
    return jax.shard_map(body, mesh=mesh, in_specs=in_specs, out_specs=out_specs, check_vma=False)
```
